32 devices in a mesh: ref: 4 (over x, core), dom: 8 (over z, y).
Axes of the slice: x: 2, y: 2, z: 4, core: 2. Of those that a mesh axis runs over, the one named last changes fastest.
Arguments:
- particles: bfloat16 [512, 7168], P(('ref', 'dom')), may hold values from -16 to 16
- offsets: int32 [512], P(('ref', 'dom')), may hold values from 0 to 8, as said below
- references: bfloat16 [512, 7168], P('ref'), may hold values from -0.6 to 0.6
- noise_weight: float32 [3584], replicated, may hold values from 0.06 to 0.24
- ref_class: int32 [512], replicated, may hold values from 0 to 7
- ref_orient: int32 [512], replicated, may hold values from 0 to 63
- class_logprior: float32 [8], replicated, may hold values from -1 to 1
- orient_logprior: float32 [64], replicated, may hold values from -1 to 1
Outputs:
- log_post: float32 [512, 9, 512], P(('ref', 'dom'))
- class_sums: float32 [8, 7168], P(None, ('ref', 'dom'))
The draws below stay inside these ranges and needn't reach their ends.
Inputs may be any that keep to these rules, and one draw needn't show every extreme that they name: `offsets`: index of the prior's centre: horizontal step (o mod 3) - 1 pixels, vertical step floor(o / 3) - 1 pixels.
All inputs are finite; a program needn't handle non-finite values.
Results may differ from the reference program's by a relative error of at most 0.0042.
Values may be sent and summed in bfloat16 or wider, within the bound.
No kernel may reach another device: no remote copies, remote signals or barrier semaphores. Data moves between devices by JAX's collectives and lax.ppermute only.
A program may use at most 64 MiB of HBM per device.

```python
import math
import jax
import jax.numpy as jnp
from jax import lax

K = 3584
CLASSES = 8
ORIENT = 64
SHIFTS = 9
REFS = 512
NPART = 512


def shared_draw(key):
    ref_key = jax.random.fold_in(key, 101)
    offset_key = jax.random.fold_in(key, 102)
    ref_values = 0.1 * jnp.clip(jax.random.normal(ref_key, (REFS, 2 * K), jnp.float32), -6.0, 6.0)
    offset_values = jax.random.randint(offset_key, (NPART,), 0, SHIFTS, dtype=jnp.int32)
    return (ref_values, offset_values)


def draw_references(key, part):
    ref_values, offset_values = shared_draw(key)
    return ref_values.astype(jnp.bfloat16)


def draw_offsets(key, part):
    ref_values, offset_values = shared_draw(key)
    return offset_values


def draw_particles(key, part):
    noise_key = jax.random.fold_in(key, 103)
    drawn = jnp.clip(jax.random.normal(noise_key, (NPART, 2 * K), jnp.float32), -6.0, 6.0)
    return drawn.astype(jnp.bfloat16)


def with_ends(result, own_key, least, top_value):
    longest = result.shape.index(max(result.shape))
    spots = []
    for shift in (0, 1):
        where = [jax.random.randint(jax.random.fold_in(own_key, axis), (), 0, length) for axis, length in enumerate(result.shape)]
        where[longest] = (where[longest] + shift) % result.shape[longest]
        spots.append(tuple(where))
    return result.at[spots[0]].set(least).at[spots[1]].set(top_value)


def setup_inputs(seed: int = 0) -> dict:
    key_of = jax.random.split(jax.random.key(seed), 9)
    return {
        "particles": draw_particles(jax.random.fold_in(key_of[8], 71), 0),
        "offsets": draw_offsets(jax.random.fold_in(key_of[8], 71), 0),
        "references": draw_references(jax.random.fold_in(key_of[8], 71), 0),
        "noise_weight": jnp.clip(jnp.exp(jax.random.uniform(key_of[3], (K,), jnp.float32, math.log(0.06), math.log(0.24))), 0.06, 0.24),
        "ref_class": with_ends(jax.random.randint(key_of[4], (REFS,), 0, CLASSES), jax.random.fold_in(key_of[4], 1), 0, CLASSES - 1).astype(jnp.int32),
        "ref_orient": with_ends(jax.random.randint(key_of[5], (REFS,), 0, ORIENT), jax.random.fold_in(key_of[5], 1), 0, ORIENT - 1).astype(jnp.int32),
        "class_logprior": jnp.clip(jax.random.uniform(key_of[6], (CLASSES,), jnp.float32, -1.0, 1.0), -1.0, 1.0),
        "orient_logprior": jnp.clip(jax.random.uniform(key_of[7], (ORIENT,), jnp.float32, -1.0, 1.0), -1.0, 1.0),
    }


def shift_tables(count):
    coeffs = jnp.arange(count, dtype=jnp.int32)
    column_freq = (coeffs % 56).astype(jnp.float32)
    row_freq = (coeffs // 56 - 32).astype(jnp.float32)
    shift_ids = jnp.arange(SHIFTS, dtype=jnp.int32)
    step_right = (shift_ids % 3 - 1).astype(jnp.float32)
    step_down = (shift_ids // 3 - 1).astype(jnp.float32)
    turning = 2.0 * math.pi / 96.0 * (step_right[:, None] * column_freq[None, :] + step_down[:, None] * row_freq[None, :])
    return (jnp.cos(turning), jnp.sin(turning))

def centre_prior(offsets):
    shift_ids = jnp.arange(SHIFTS, dtype=jnp.int32)
    step_right = (shift_ids % 3 - 1).astype(jnp.float32)
    step_down = (shift_ids // 3 - 1).astype(jnp.float32)
    centre_right = (offsets % 3 - 1).astype(jnp.float32)
    centre_down = (offsets // 3 - 1).astype(jnp.float32)
    apart_right = step_right[None, :] - centre_right[:, None]
    apart_down = step_down[None, :] - centre_down[:, None]
    return -0.5 * (apart_right * apart_right + apart_down * apart_down)

def aligned_stack(real_part, imag_part, cosine_table, sine_table, twice):
    turned_real = real_part[:, None, :] * cosine_table[None] - imag_part[:, None, :] * sine_table[None]
    turned_imag = real_part[:, None, :] * sine_table[None] + imag_part[:, None, :] * cosine_table[None]
    stacked_rows = real_part.shape[0] * cosine_table.shape[0]
    scaled_real = (turned_real * twice[None, None, :]).astype(jnp.bfloat16).reshape(stacked_rows, real_part.shape[1])
    scaled_imag = (turned_imag * twice[None, None, :]).astype(jnp.bfloat16).reshape(stacked_rows, real_part.shape[1])
    return (scaled_real, scaled_imag)

def reference(particles, offsets, references, noise_weight, ref_class, ref_orient, class_logprior, orient_logprior):
    cosine_table, sine_table = shift_tables(K)
    twice = 2.0 * noise_weight
    refs_wide = references.astype(jnp.float32)
    ref_norm = lax.optimization_barrier(jnp.sum(noise_weight[None, :] * (refs_wide[:, :K] * refs_wide[:, :K] + refs_wide[:, K:] * refs_wide[:, K:]), axis=1))
    class_table = (ref_class[:, None] == jnp.arange(CLASSES, dtype=jnp.int32)[None, :]).astype(jnp.float32)
    orient_table = (ref_orient[:, None] == jnp.arange(ORIENT, dtype=jnp.int32)[None, :]).astype(jnp.float32)
    prior = jnp.dot(class_table, class_logprior, precision=lax.Precision.HIGHEST) + jnp.dot(orient_table, orient_logprior, precision=lax.Precision.HIGHEST)
    block_rows = math.gcd(NPART, 1024)
    nblocks = NPART // block_rows
    stacked = particles.reshape(nblocks, block_rows, 2 * K)
    stacked_offsets = offsets.reshape(nblocks, block_rows)

    def visit(running, inputs):
        block, block_offsets = inputs
        values = block.astype(jnp.float32)
        real_part = values[:, :K]
        imag_part = values[:, K:]
        scaled_real, scaled_imag = aligned_stack(real_part, imag_part, cosine_table, sine_table, twice)
        cross = jnp.dot(scaled_real, references[:, :K].T, preferred_element_type=jnp.float32) + jnp.dot(scaled_imag, references[:, K:].T, preferred_element_type=jnp.float32)
        scores = cross.reshape(block_rows, SHIFTS, REFS) - ref_norm[None, None, :] + prior[None, None, :] + centre_prior(block_offsets)[:, :, None]
        row_peak = lax.optimization_barrier(jnp.max(scores, axis=(1, 2), keepdims=True))
        log_total = row_peak + jnp.log(lax.optimization_barrier(jnp.sum(jnp.exp(scores - row_peak), axis=(1, 2), keepdims=True)))
        log_post = scores - log_total
        class_post = jnp.dot(jnp.exp(log_post).reshape(block_rows * SHIFTS, REFS), class_table, precision=lax.Precision.HIGHEST).reshape(block_rows, SHIFTS, CLASSES)
        sums_real = jnp.einsum('ntc,nk->tck', class_post, real_part, precision=lax.Precision.HIGHEST)
        sums_imag = jnp.einsum('ntc,nk->tck', class_post, imag_part, precision=lax.Precision.HIGHEST)
        return ((running[0] + sums_real, running[1] + sums_imag), log_post)
    initial = (jnp.zeros((SHIFTS, CLASSES, K), jnp.float32), jnp.zeros((SHIFTS, CLASSES, K), jnp.float32))
    running, posts = lax.scan(visit, initial, (stacked, stacked_offsets))
    sums_real, sums_imag = running
    class_real = jnp.einsum('tk,tck->ck', cosine_table, sums_real, precision=lax.Precision.HIGHEST) - jnp.einsum('tk,tck->ck', sine_table, sums_imag, precision=lax.Precision.HIGHEST)
    class_imag = jnp.einsum('tk,tck->ck', sine_table, sums_real, precision=lax.Precision.HIGHEST) + jnp.einsum('tk,tck->ck', cosine_table, sums_imag, precision=lax.Precision.HIGHEST)
    class_sums = jnp.concatenate([class_real, class_imag], axis=1) * (1.0 / math.sqrt(NPART))
    return (posts.reshape(NPART, SHIFTS, REFS), class_sums)
```

```python
import functools
import math

import jax
import jax.numpy as jnp
import numpy as np
from jax import lax
from jax.experimental import pallas as pl
from jax.experimental.pallas import tpu as pltpu
from jax.sharding import PartitionSpec as P

SHIFTS = 9
PAIRS = 4
LANES = 128
CHUNK = 512
VMEM_LIMIT = 24 * 1024 * 1024


def turning_table(count):
    coeffs = np.arange(count)
    column_freq = (coeffs % 56).astype(np.float32)
    row_freq = (coeffs // 56 - 32).astype(np.float32)
    shift_ids = np.arange(SHIFTS - PAIRS, SHIFTS)
    right = (shift_ids % 3 - 1).astype(np.float32)
    down = (shift_ids // 3 - 1).astype(np.float32)
    turning = np.float32(2.0 * math.pi / 96.0) * (
        right[:, None] * column_freq[None, :] + down[:, None] * row_freq[None, :]
    )
    return np.concatenate([np.cos(turning), np.sin(turning)], axis=0).astype(np.float32)


def three_parts(value):
    high = value.astype(jnp.bfloat16)
    rest = value - high.astype(jnp.float32)
    middle = rest.astype(jnp.bfloat16)
    low = (rest - middle.astype(jnp.float32)).astype(jnp.bfloat16)
    return high, middle, low


def chunks(total):
    size = CHUNK if total % CHUNK == 0 else LANES
    return [(start, size) for start in range(0, total, size)]


def dot_nt(left, right):
    return lax.dot_general(
        left, right, (((1,), (1,)), ((), ())), preferred_element_type=jnp.float32
    )


def score_body(first, classes, own_ref, peer_ref, part_ref, table_ref, weight_ref, bias_ref,
               class_ref, tag_ref, scores_ref, stats_ref, bias_out_ref=None):
    rows, width = part_ref.shape
    coefs = width // 2
    block = own_ref.shape[0]
    cross = jnp.zeros((SHIFTS * rows, 2 * block), jnp.float32)
    norm = jnp.zeros((2 * block, LANES), jnp.float32)
    for start, size in chunks(coefs):
        re = pl.ds(start, size)
        im = pl.ds(coefs + start, size)
        weight = weight_ref[:, re]
        twice = 2.0 * weight
        table = table_ref[:, re] * twice
        x = part_ref[:, re].astype(jnp.float32)
        y = part_ref[:, im].astype(jnp.float32)
        real = [None] * SHIFTS
        imag = [None] * SHIFTS
        middle = SHIFTS // 2
        real[middle] = (x * twice).astype(jnp.bfloat16)
        imag[middle] = (y * twice).astype(jnp.bfloat16)
        for p in range(PAIRS):
            cosine = table[p : p + 1]
            sine = table[PAIRS + p : PAIRS + p + 1]
            xc, ys, xs, yc = x * cosine, y * sine, x * sine, y * cosine
            t = middle + 1 + p
            real[t] = (xc - ys).astype(jnp.bfloat16)
            imag[t] = (xs + yc).astype(jnp.bfloat16)
            real[SHIFTS - 1 - t] = (xc + ys).astype(jnp.bfloat16)
            imag[SHIFTS - 1 - t] = (yc - xs).astype(jnp.bfloat16)
        refs_re = jnp.concatenate([own_ref[:, re], peer_ref[:, re]], axis=0)
        refs_im = jnp.concatenate([own_ref[:, im], peer_ref[:, im]], axis=0)
        cross += dot_nt(jnp.concatenate(real, axis=0), refs_re)
        cross += dot_nt(jnp.concatenate(imag, axis=0), refs_im)
        if first:
            for lane in range(0, size, LANES):
                a = refs_re[:, lane : lane + LANES].astype(jnp.float32)
                b = refs_im[:, lane : lane + LANES].astype(jnp.float32)
                norm += weight[:, lane : lane + LANES] * (a * a + b * b)
    bias = bias_ref[...]
    if first:
        bias = bias - jnp.sum(jnp.transpose(norm), axis=0, keepdims=True)
        bias_out_ref[...] = bias
    scores = cross + bias
    scores_ref[...] = scores.reshape(SHIFTS, rows, 2 * block)
    peak = scores[:rows]
    for t in range(1, SHIFTS):
        peak = jnp.maximum(peak, scores[t * rows : (t + 1) * rows])
    peak = jnp.max(peak, axis=1, keepdims=True)
    mass = jnp.exp(scores - jnp.concatenate([peak] * SHIFTS, axis=0))
    lanes = lax.broadcasted_iota(jnp.int32, (2 * block, LANES), 1)
    table = (lanes == class_ref[...]).astype(jnp.float32).astype(jnp.bfloat16)
    high, mid, low = three_parts(mass)
    by_class = jnp.dot(jnp.concatenate([high, mid, low], axis=0), table,
                       preferred_element_type=jnp.float32)
    span = SHIFTS * rows
    by_class = by_class[:span] + by_class[span : 2 * span] + by_class[2 * span :]
    stats = by_class[:rows]
    for t in range(1, SHIFTS):
        stats += pltpu.roll(by_class[t * rows : (t + 1) * rows], classes * t, 1)
    lane = lax.broadcasted_iota(jnp.int32, (rows, LANES), 1)
    stats = jnp.where(lane == SHIFTS * classes, peak, stats)
    stats = jnp.where(lane == SHIFTS * classes + 1, tag_ref[...], stats)
    stats_ref[...] = stats


def score(first, classes, own, peer, part, table, weight, bias, class_col, tag):
    rows, width = part.shape
    block = own.shape[0]
    outs = [
        jax.ShapeDtypeStruct((SHIFTS, rows, 2 * block), jnp.float32),
        jax.ShapeDtypeStruct((rows, LANES), jnp.float32),
    ]
    if first:
        outs.append(jax.ShapeDtypeStruct((1, 2 * block), jnp.float32))
    flops = 2 * SHIFTS * rows * width * 2 * block
    return pl.pallas_call(
        functools.partial(score_body, first, classes),
        out_shape=outs,
        name="score_own" if first else "score_other",
        compiler_params=pltpu.CompilerParams(vmem_limit_bytes=VMEM_LIMIT),
        cost_estimate=pl.CostEstimate(
            flops=flops, bytes_accessed=2 * (2 * block + rows) * width, transcendentals=0
        ),
    )(own, peer, part, table, weight, bias, class_col, tag)


def sums_body(groups, classes, scale, place_ref, table_ref, *refs):
    stats = refs[:groups]
    parts = refs[groups : 2 * groups]
    keep_ref, send_ref, total_ref = refs[2 * groups :]
    rows = parts[0].shape[0]
    width = parts[0].shape[1]
    coefs = width // 2
    span = width // groups
    used = SHIFTS * classes
    chip, core, dom = place_ref[0], place_ref[1], place_ref[2]
    lane = lax.broadcasted_iota(jnp.int32, (rows, LANES), 1)
    shift = lane // classes
    right = (shift % 3 - 1).astype(jnp.float32)
    down = (shift // 3 - 1).astype(jnp.float32)
    posts = []
    for slot in range(groups):
        seen = [stats[i][(slot ^ i) * rows : ((slot ^ i) + 1) * rows] for i in range(groups)]
        peaks = [value[:, used : used + 1] for value in seen]
        peak = functools.reduce(jnp.maximum, peaks)
        mass = sum(value * jnp.exp(low - peak) for value, low in zip(seen, peaks))
        centre = stats[slot][:rows, used + 1 : used + 2].astype(jnp.int32)
        across = right - (centre % 3 - 1).astype(jnp.float32)
        along = down - (centre // 3 - 1).astype(jnp.float32)
        prior = -0.5 * (across * across + along * along)
        mass = jnp.where(lane < used, mass * jnp.exp(prior), 0.0)
        whole = jnp.sum(mass, axis=1, keepdims=True)
        posts.append(mass / whole)
        if slot == 0:
            total_ref[...] = prior - (peak + jnp.log(whole))
    post = jnp.transpose(jnp.concatenate(posts, axis=0))
    middle = SHIFTS // 2
    by_shift = [post[t * classes : (t + 1) * classes] for t in range(SHIFTS)]
    even = [by_shift[middle]]
    odd = []
    for p in range(PAIRS):
        t = middle + 1 + p
        even.append(by_shift[t] + by_shift[SHIFTS - 1 - t])
        odd.append(by_shift[t] - by_shift[SHIFTS - 1 - t])
    even = jnp.concatenate(three_parts(jnp.concatenate(even, axis=0)), axis=0)
    odd = jnp.concatenate(three_parts(jnp.concatenate(odd, axis=0)), axis=0)
    sign = jnp.where(chip < groups // 2, -1.0, 1.0)
    column = chip * span
    other = lax.rem(column + coefs, width)
    base = lax.rem(column, coefs)
    step = CHUNK if span % CHUNK == 0 else LANES
    pieces = []
    for start in range(0, span, step):
        u = jnp.concatenate(
            [part[:, pl.ds(pl.multiple_of(column + start, LANES), step)] for part in parts], axis=0
        )
        v = jnp.concatenate(
            [part[:, pl.ds(pl.multiple_of(other + start, LANES), step)] for part in parts], axis=0
        )
        table = table_ref[:, pl.ds(pl.multiple_of(base + start, LANES), step)]
        evens = jnp.dot(even, u, preferred_element_type=jnp.float32)
        odds = jnp.dot(odd, v, preferred_element_type=jnp.float32)
        ne = (PAIRS + 1) * classes
        no = PAIRS * classes
        evens = evens[:ne] + (evens[ne : 2 * ne] + evens[2 * ne :])
        odds = odds[:no] + (odds[no : 2 * no] + odds[2 * no :])
        direct = evens[:classes]
        turned = jnp.zeros_like(direct)
        for p in range(PAIRS):
            direct += table[p : p + 1] * evens[(p + 1) * classes : (p + 2) * classes]
            turned += table[PAIRS + p : PAIRS + p + 1] * odds[p * classes : (p + 1) * classes]
        pieces.append((direct + sign * turned) * scale)
    result = jnp.concatenate(pieces, axis=1)
    slots = keep_ref.shape[0]
    part_width = keep_ref.shape[2]
    for half in range(2):
        for d in range(slots):
            at = (half * slots + d) * part_width
            piece = result[:, at : at + part_width]

            @pl.when(core == half)
            def _(piece=piece, d=d):
                keep_ref[lax.bitwise_xor(dom, d)] = piece

            @pl.when(core != half)
            def _(piece=piece, d=d):
                send_ref[lax.bitwise_xor(dom, d)] = piece


def partial_sums(groups, classes, scale, slots, columns, place, table, stats, parts):
    rows = parts[0].shape[0]
    piece = jax.ShapeDtypeStruct((slots, classes, columns), jnp.float32)
    vmem = pl.BlockSpec(memory_space=pltpu.VMEM)
    return pl.pallas_call(
        functools.partial(sums_body, groups, classes, scale),
        out_shape=[piece, piece, jax.ShapeDtypeStruct((rows, LANES), jnp.float32)],
        in_specs=[pl.BlockSpec(memory_space=pltpu.SMEM)] + [vmem] * (1 + 2 * groups),
        out_specs=[vmem] * 3,
        name="class_partial",
        compiler_params=pltpu.CompilerParams(vmem_limit_bytes=VMEM_LIMIT),
        cost_estimate=pl.CostEstimate(flops=1000000, bytes_accessed=1000000, transcendentals=0),
    )(place, table, *stats, *parts)


def local(refs_axis, dom_axis, particles, offsets, references, noise_weight, ref_class, ref_orient,
          class_logprior, orient_logprior):
    rows, width = particles.shape
    coefs = width // 2
    block = references.shape[0]
    classes = class_logprior.shape[0]
    groups = refs_axis // 2
    me = lax.axis_index("ref")
    dom = lax.axis_index("dom")

    def swap(value, axis, size, bit):
        return lax.ppermute(value, axis, [(i, i ^ bit) for i in range(size)])

    others = [swap(particles, "ref", refs_axis, 2 * i) for i in range(1, groups)]
    peer_refs = swap(references, "ref", refs_axis, 1)

    table = jnp.asarray(turning_table(coefs))
    weight = noise_weight[None, :]
    class_row = jnp.sum(
        jnp.where(jnp.arange(classes)[:, None] == ref_class[None, :], class_logprior[:, None], 0.0),
        axis=0,
    )
    orient_row = jnp.sum(
        jnp.where(
            jnp.arange(orient_logprior.shape[0])[:, None] == ref_orient[None, :],
            orient_logprior[:, None],
            0.0,
        ),
        axis=0,
    )
    prior = class_row + orient_row

    def mine(row):
        return jnp.concatenate(
            [lax.dynamic_slice(row, ((me ^ i) * block,), (block,)) for i in range(2)]
        )

    bias = mine(prior)[None, :]
    class_col = mine(ref_class)[:, None]
    tag = offsets.astype(jnp.float32)[:, None]
    fixed = (references, peer_refs)
    own_scores, own_stats, bias = score(
        True, classes, *fixed, particles, table, weight, bias, class_col, tag
    )
    sent_scores, stats = [], [own_stats]
    for other in others:
        value, stat = score(False, classes, *fixed, other, table, weight, bias, class_col, tag)
        sent_scores.append(value)
        stats.append(stat)
    stats = jnp.concatenate(stats, axis=0)
    seen = [stats] + [swap(stats, "ref", refs_axis, 2 * i) for i in range(1, groups)]
    place = jnp.stack([me // 2, me % 2, dom]).astype(jnp.int32)
    scale = 1.0 / math.sqrt(rows * refs_axis * dom_axis)
    columns = width // (refs_axis * dom_axis)
    keep, send, total = partial_sums(
        groups, classes, scale, dom_axis, columns, place, table, seen, [particles] + others
    )
    keep = keep + swap(send, "ref", refs_axis, 1)
    slots = dom_axis
    while slots > 1:
        slots //= 2
        keep = keep[:slots] + swap(keep[slots:], "dom", dom_axis, slots)
    class_sums = keep[0]

    got = [own_scores] + [
        swap(value, "ref", refs_axis, 2 * (i + 1)) for i, value in enumerate(sent_scores)
    ]
    blocks = []
    for value in got:
        blocks += [value[:, :, :block], value[:, :, block:]]
    bit = 1
    while bit < refs_axis:
        blocks = [
            jnp.where((me & bit) != 0, blocks[j ^ bit], blocks[j]) for j in range(refs_axis)
        ]
        bit *= 2
    lift = jnp.transpose(total[:, : SHIFTS * classes].reshape(rows, SHIFTS, classes)[:, :, 0])
    log_post = jnp.concatenate(blocks, axis=2) + lift[:, :, None]
    return (jnp.transpose(log_post, (1, 0, 2)), class_sums)


def solution(mesh):
    return jax.shard_map(
        functools.partial(local, mesh.shape["ref"], mesh.shape["dom"]),
        mesh=mesh,
        in_specs=(
            P(("ref", "dom"), None),
            P(("ref", "dom")),
            P("ref", None),
            P(),
            P(),
            P(),
            P(),
            P(),
        ),
        out_specs=(P(("ref", "dom"), None, None), P(None, ("ref", "dom"))),
        check_vma=False,
    )
```

```python
import functools
import math

import jax
import jax.numpy as jnp
import numpy as np
from jax import lax
from jax.experimental import pallas as pl
from jax.experimental.pallas import tpu as pltpu
from jax.sharding import PartitionSpec as P

SHIFTS = 9
PAIRS = 4
LANES = 128
CHUNK = 512
VMEM_LIMIT = 24 * 1024 * 1024


def turning_table(count):
    coeffs = np.arange(count)
    column_freq = (coeffs % 56).astype(np.float32)
    row_freq = (coeffs // 56 - 32).astype(np.float32)
    shift_ids = np.arange(SHIFTS - PAIRS, SHIFTS)
    right = (shift_ids % 3 - 1).astype(np.float32)
    down = (shift_ids // 3 - 1).astype(np.float32)
    turning = np.float32(2.0 * math.pi / 96.0) * (
        right[:, None] * column_freq[None, :] + down[:, None] * row_freq[None, :]
    )
    return np.concatenate([np.cos(turning), np.sin(turning)], axis=0).astype(np.float32)


def chunks(total):
    size = CHUNK if total % CHUNK == 0 else LANES
    return [(start, size) for start in range(0, total, size)]


def dot_nt(left, right):
    return lax.dot_general(
        left, right, (((1,), (1,)), ((), ())), preferred_element_type=jnp.float32
    )


def two_parts(value):
    high = value.astype(jnp.bfloat16)
    low = (value - high.astype(jnp.float32)).astype(jnp.bfloat16)
    return [high, low]


def cross_terms(ref_blocks, part_ref, table_ref, weight_ref, want_norm, arriving=()):
    rows, width = part_ref.shape
    coefs = width // 2
    count = sum(block.shape[0] for block in ref_blocks)
    cross = jnp.zeros((SHIFTS * rows, count), jnp.float32)
    norm = jnp.zeros((count, LANES), jnp.float32)
    middle = SHIFTS // 2
    for i, (start, size) in enumerate(chunks(coefs)):
        for copy in arriving[i] if arriving else ():
            copy.wait()
        re = pl.ds(start, size)
        im = pl.ds(coefs + start, size)
        row = start // LANES
        weight = jnp.concatenate(
            [weight_ref[row + j : row + j + 1, :] for j in range(size // LANES)], axis=1
        )
        twice = 2.0 * weight
        table = table_ref[:, re] * twice
        x = part_ref[:, re].astype(jnp.float32)
        y = part_ref[:, im].astype(jnp.float32)
        real = [None] * SHIFTS
        imag = [None] * SHIFTS
        real[middle] = (x * twice).astype(jnp.bfloat16)
        imag[middle] = (y * twice).astype(jnp.bfloat16)
        for p in range(PAIRS):
            cosine = table[p : p + 1]
            sine = table[PAIRS + p : PAIRS + p + 1]
            xc, ys, xs, yc = x * cosine, y * sine, x * sine, y * cosine
            t = middle + 1 + p
            real[t] = (xc - ys).astype(jnp.bfloat16)
            imag[t] = (xs + yc).astype(jnp.bfloat16)
            real[SHIFTS - 1 - t] = (xc + ys).astype(jnp.bfloat16)
            imag[SHIFTS - 1 - t] = (yc - xs).astype(jnp.bfloat16)
        refs_re = jnp.concatenate([block[:, re] for block in ref_blocks], axis=0)
        refs_im = jnp.concatenate([block[:, im] for block in ref_blocks], axis=0)
        cross += dot_nt(jnp.concatenate(real, axis=0), refs_re)
        cross += dot_nt(jnp.concatenate(imag, axis=0), refs_im)
        if want_norm:
            for lane in range(0, size, LANES):
                a = refs_re[:, lane : lane + LANES].astype(jnp.float32)
                b = refs_im[:, lane : lane + LANES].astype(jnp.float32)
                norm += weight[:, lane : lane + LANES] * (a * a + b * b)
    return cross, norm


def block_prior(index, class_ref, orient_ref, class_prior_ref, orient_prior_ref):
    kind = class_ref[pl.ds(index, 1), :]
    orient = orient_ref[pl.ds(index, 1), :]
    first = jnp.zeros(kind.shape, jnp.float32)
    second = jnp.zeros(kind.shape, jnp.float32)
    for c in range(class_prior_ref.shape[0]):
        first = jnp.where(kind == c, class_prior_ref[c], first)
    for o in range(orient_prior_ref.shape[0]):
        second = jnp.where(orient == o, orient_prior_ref[o], second)
    return first + second


def statistics(classes, me, blocks, class_ref, tag):
    scores = jnp.concatenate(blocks, axis=1)
    rows = scores.shape[0] // SHIFTS
    peak = scores[:rows]
    for t in range(1, SHIFTS):
        peak = jnp.maximum(peak, scores[t * rows : (t + 1) * rows])
    peak = jnp.max(peak, axis=1, keepdims=True)
    mass = jnp.exp(scores - jnp.concatenate([peak] * SHIFTS, axis=0))
    kind = jnp.concatenate(
        [class_ref[pl.ds(me, 1), :], class_ref[pl.ds(lax.bitwise_xor(me, 1), 1), :]], axis=1
    )
    want = lax.rem(lax.broadcasted_iota(jnp.int32, (LANES, scores.shape[1]), 0), classes)
    table = jnp.where(want == kind, 1.0, 0.0).astype(jnp.bfloat16)
    span = SHIFTS * rows
    by_class = dot_nt(jnp.concatenate(two_parts(mass), axis=0), table)
    by_class = by_class[:span] + by_class[span:]
    lane = lax.broadcasted_iota(jnp.int32, (rows, LANES), 1)
    shift = lane // classes
    stats = jnp.where(lane == SHIFTS * classes, peak, 0.0)
    if tag is not None:
        stats = jnp.where(lane == SHIFTS * classes + 1, tag, stats)
    for t in range(SHIFTS):
        stats = jnp.where(shift == t, by_class[t * rows : (t + 1) * rows], stats)
    return stats


def near_body(classes, refs_hbm, part_hbm, table_hbm, weight_hbm, class_hbm, orient_hbm,
              class_prior_hbm, orient_prior_hbm, offset_hbm, scores_ref, bias_ref, tag_ref,
              refs_ref, part_ref, table_ref, weight_ref, class_ref,
              orient_ref, class_prior_ref, orient_prior_ref, offset_ref, small_sems, refs_sems):
    me = lax.axis_index("ref")
    coefs = part_ref.shape[1] // 2
    small = [
        pltpu.make_async_copy(source, target, small_sems.at[i])
        for i, (source, target) in enumerate(
            [
                (part_hbm, part_ref), (table_hbm, table_ref), (weight_hbm, weight_ref),
                (class_hbm, class_ref), (orient_hbm, orient_ref),
                (class_prior_hbm, class_prior_ref), (orient_prior_hbm, orient_prior_ref),
                (offset_hbm, offset_ref),
            ]
        )
    ]
    for copy in small:
        copy.start()
    arriving = []
    for i, (start, size) in enumerate(chunks(coefs)):
        pair = []
        for j in range(2):
            columns = pl.ds(j * coefs + start, size)
            pair.append(
                pltpu.make_async_copy(
                    refs_hbm.at[:, columns], refs_ref.at[:, columns], refs_sems.at[2 * i + j]
                )
            )
        for copy in pair:
            copy.start()
        arriving.append(pair)
    for copy in small:
        copy.wait()
    rows = part_ref.shape[0]
    row = lax.broadcasted_iota(jnp.int32, (rows, LANES), 0)
    tag = jnp.zeros((rows, LANES), jnp.int32)
    for i in range(rows):
        tag = jnp.where(row == i, offset_ref[i], tag)
    tag_ref[...] = tag.astype(jnp.float32)
    cross, norm = cross_terms([refs_ref], part_ref, table_ref, weight_ref, True, arriving)
    priors = [
        block_prior(
            lax.bitwise_xor(me, i), class_ref, orient_ref, class_prior_ref, orient_prior_ref
        )
        for i in range(2)
    ]
    bias = priors[0] - jnp.sum(jnp.transpose(norm), axis=0, keepdims=True)
    bias_ref[0:1, :] = bias
    bias_ref[1:2, :] = priors[1]
    scores_ref[...] = (cross + bias).reshape(scores_ref.shape)


def pair_body(classes, near_ref, peer_ref, part_ref, table_ref, weight_ref, class_ref, prior_ref,
              tag_ref, scores_ref, bias_ref, stats_ref):
    me = lax.axis_index("ref")
    cross, norm = cross_terms([peer_ref], part_ref, table_ref, weight_ref, True)
    bias = prior_ref[1:2, :] - jnp.sum(jnp.transpose(norm), axis=0, keepdims=True)
    bias_ref[0:1, :] = prior_ref[0:1, :]
    bias_ref[1:2, :] = bias
    scores = cross + bias
    scores_ref[...] = scores.reshape(scores_ref.shape)
    near = near_ref[...].reshape(scores.shape)
    stats_ref[...] = statistics(classes, me, [near, scores], class_ref, tag_ref[...])


def far_body(classes, own_ref, peer_ref, part_ref, table_ref, weight_ref, class_ref, bias_ref,
             scores_ref, stats_ref):
    me = lax.axis_index("ref")
    block = own_ref.shape[0]
    cross, _ = cross_terms([own_ref, peer_ref], part_ref, table_ref, weight_ref, False)
    blocks = [cross[:, i * block : (i + 1) * block] + bias_ref[i : i + 1, :] for i in range(2)]
    stats_ref[...] = statistics(classes, me, blocks, class_ref, None)
    for i in range(2):
        scores_ref[:, :, i * block : (i + 1) * block] = blocks[i].reshape(
            scores_ref.shape[0], scores_ref.shape[1], block
        )


VMEM = pl.BlockSpec(memory_space=pltpu.VMEM)
HBM = pl.BlockSpec(memory_space=pltpu.HBM)


def call(body, name, shapes, specs, cost, *operands, scratch=()):
    return pl.pallas_call(
        body,
        out_shape=[
            shape if isinstance(shape, jax.ShapeDtypeStruct)
            else jax.ShapeDtypeStruct(shape, jnp.float32)
            for shape in shapes
        ],
        scratch_shapes=scratch,
        in_specs=specs,
        out_specs=[VMEM] * len(shapes),
        name=name,
        compiler_params=pltpu.CompilerParams(vmem_limit_bytes=VMEM_LIMIT),
        cost_estimate=pl.CostEstimate(
            flops=int(cost * 5e8), bytes_accessed=int(cost * 1e6), transcendentals=0
        ),
    )(*operands)


def sums_body(groups, classes, scale, table_ref, *refs):
    stats = refs[:groups]
    parts = refs[groups : 2 * groups]
    sums_ref, total_ref = refs[2 * groups :]
    rows = parts[0].shape[0]
    width = parts[0].shape[1]
    coefs = width // 2
    span = width // groups
    used = SHIFTS * classes
    me = lax.axis_index("ref")
    dom = lax.axis_index("dom")
    chip, core = me // 2, lax.rem(me, 2)
    lane = lax.broadcasted_iota(jnp.int32, (rows, LANES), 1)
    shift = lane // classes
    right = (shift % 3 - 1).astype(jnp.float32)
    down = (shift // 3 - 1).astype(jnp.float32)
    posts = []
    for slot in range(groups):
        seen = [stats[i][(slot ^ i) * rows : ((slot ^ i) + 1) * rows] for i in range(groups)]
        peaks = [value[:, used : used + 1] for value in seen]
        peak = functools.reduce(jnp.maximum, peaks)
        mass = sum(value * jnp.exp(low - peak) for value, low in zip(seen, peaks))
        centre = stats[slot][:rows, used + 1 : used + 2].astype(jnp.int32)
        across = right - (centre % 3 - 1).astype(jnp.float32)
        along = down - (centre // 3 - 1).astype(jnp.float32)
        prior = -0.5 * (across * across + along * along)
        mass = jnp.where(lane < used, mass * jnp.exp(prior), 0.0)
        whole = jnp.sum(mass, axis=1, keepdims=True)
        posts.append(mass / whole)
        if slot == 0:
            total_ref[...] = prior - (peak + jnp.log(whole))
    post = jnp.transpose(jnp.concatenate(posts, axis=0)) * scale
    middle = SHIFTS // 2
    by_shift = [post[t * classes : (t + 1) * classes] for t in range(SHIFTS)]
    even = [by_shift[middle]]
    odd = []
    sign = jnp.where(chip < groups // 2, -1.0, 1.0)
    for p in range(PAIRS):
        t = middle + 1 + p
        even.append(by_shift[t] + by_shift[SHIFTS - 1 - t])
        odd.append(sign * (by_shift[t] - by_shift[SHIFTS - 1 - t]))
    even = jnp.concatenate(two_parts(jnp.concatenate(even, axis=0)), axis=0)
    odd = jnp.concatenate(two_parts(jnp.concatenate(odd, axis=0)), axis=0)
    column = chip * span
    other = lax.rem(column + coefs, width)
    base = lax.rem(column, coefs)
    step = CHUNK if span % CHUNK == 0 else LANES
    ne = (PAIRS + 1) * classes
    no = PAIRS * classes
    pieces = []
    for start in range(0, span, step):
        u = jnp.concatenate(
            [part[:, pl.ds(pl.multiple_of(column + start, LANES), step)] for part in parts], axis=0
        )
        v = jnp.concatenate(
            [part[:, pl.ds(pl.multiple_of(other + start, LANES), step)] for part in parts], axis=0
        )
        table = table_ref[:, pl.ds(pl.multiple_of(base + start, LANES), step)]
        evens = jnp.dot(even, u, preferred_element_type=jnp.float32)
        odds = jnp.dot(odd, v, preferred_element_type=jnp.float32)
        evens = evens[:ne] + evens[ne:]
        odds = odds[:no] + odds[no:]
        result = evens[:classes]
        for p in range(PAIRS):
            result += table[p : p + 1] * evens[(p + 1) * classes : (p + 2) * classes]
            result += table[PAIRS + p : PAIRS + p + 1] * odds[p * classes : (p + 1) * classes]
        pieces.append(result)
    result = jnp.concatenate(pieces, axis=1)
    slots = sums_ref.shape[1]
    columns = sums_ref.shape[3]
    for half in range(2):
        for d in range(slots):
            at = (half * slots + d) * columns
            sums_ref[lax.bitwise_xor(core, half), lax.bitwise_xor(dom, d)] = result[
                :, at : at + columns
            ]


def order_body(block, groups, total_ref, *refs):
    out_ref = refs[-1]
    me = lax.axis_index("ref")
    slot = 0
    for ref in refs[:-1]:
        for at in range(0, ref.shape[2], block):
            place = pl.multiple_of(lax.bitwise_xor(me, slot) * block, LANES)
            for t in range(SHIFTS):
                lift = total_ref[:, t * groups : t * groups + 1]
                out_ref[t, :, pl.ds(place, block)] = ref[t, :, at : at + block] + lift
            slot += 1


def local(refs_axis, dom_axis, particles, offsets, references, noise_weight, ref_class, ref_orient,
          class_logprior, orient_logprior):
    rows, width = particles.shape
    coefs = width // 2
    block = references.shape[0]
    classes = class_logprior.shape[0]
    groups = refs_axis // 2
    me = lax.axis_index("ref")

    def swap(value, axis, size, bit):
        return lax.ppermute(value, axis, [(i, i ^ bit) for i in range(size)])

    with jax.named_scope("particles"):
        others = [swap(particles, "ref", refs_axis, 2 * i) for i in range(1, groups)]
    with jax.named_scope("references"):
        peer_refs = swap(references, "ref", refs_axis, 1)

    table = jnp.asarray(turning_table(coefs))
    weight = noise_weight.reshape(coefs // LANES, LANES)
    kinds = ref_class.reshape(refs_axis, block)
    orients = ref_orient.reshape(refs_axis, block)
    loaded = [references, particles, table, weight, kinds]
    near, prior, tag, *held = call(
        functools.partial(near_body, classes),
        "score_near",
        [(SHIFTS, rows, block), (2, block), (rows, LANES)]
        + [jax.ShapeDtypeStruct(value.shape, value.dtype) for value in loaded],
        [HBM] * 9,
        1.0,
        *[pltpu.with_memory_space_constraint(v, pltpu.HBM) for v in [*loaded, orients, class_logprior, orient_logprior, offsets]],
        scratch=[
            pltpu.VMEM(orients.shape, jnp.int32),
            pltpu.SMEM(class_logprior.shape, jnp.float32),
            pltpu.SMEM(orient_logprior.shape, jnp.float32),
            pltpu.SMEM(offsets.shape, jnp.int32),
            pltpu.SemaphoreType.DMA((8,)),
            pltpu.SemaphoreType.DMA((2 * len(chunks(coefs)),)),
        ],
    )
    held_refs, held_part, table, weight, kinds = held
    shared = (table, weight, kinds)
    pair, bias, own_stats = call(
        functools.partial(pair_body, classes),
        "score_pair",
        [(SHIFTS, rows, block), (2, block), (rows, LANES)],
        [VMEM] * 8,
        1.0,
        near, peer_refs, held_part, *shared, prior, tag,
    )
    sent_scores, stats = [], [own_stats]
    for other in others:
        value, stat = call(
            functools.partial(far_body, classes),
            "score_far",
            [(SHIFTS, rows, 2 * block), (rows, LANES)],
            [VMEM] * 7,
            1.0,
            held_refs, peer_refs, other, *shared, bias,
        )
        sent_scores.append(value)
        stats.append(stat)
    stats = jnp.concatenate(stats, axis=0)
    with jax.named_scope("stats"):
        seen = [stats] + [swap(stats, "ref", refs_axis, 2 * i) for i in range(1, groups)]
    with jax.named_scope("scores"):
        got = [swap(value, "ref", refs_axis, 2 * (i + 1)) for i, value in enumerate(sent_scores)]
    devices = refs_axis * dom_axis
    with jax.named_scope("partial"):
        sums, total = call(
            functools.partial(sums_body, groups, classes, 1.0 / math.sqrt(rows * devices)),
            "class_partial",
            [(2, dom_axis, classes, width // devices), (rows, LANES)],
            [VMEM] * (1 + 2 * groups),
            1.0,
            table, *seen, held_part, *others,
        )
    with jax.named_scope("halve"):
        keep = sums[0] + swap(sums[1], "ref", refs_axis, 1)
        slots = dom_axis
        while slots > 1:
            slots //= 2
            keep = keep[:slots] + swap(keep[slots:], "dom", dom_axis, slots)
        class_sums = keep[0]

    blocks = [near, pair] + got
    if block % LANES == 0:
        with jax.named_scope("order"):
            (log_post,) = call(
                functools.partial(order_body, block, classes),
                "log_post",
                [(SHIFTS, rows, refs_axis * block)],
                [VMEM] * (1 + len(blocks)),
                0.5,
                total, *blocks,
            )
    else:
        pieces = [near, pair]
        for value in got:
            pieces += [value[:, :, :block], value[:, :, block:]]
        bit = 1
        while bit < refs_axis:
            pieces = [
                jnp.where((me & bit) != 0, pieces[j ^ bit], pieces[j]) for j in range(refs_axis)
            ]
            bit *= 2
        lift = total[:, : SHIFTS * classes : classes].T
        log_post = jnp.concatenate(pieces, axis=2) + lift[:, :, None]
    return (jnp.transpose(log_post, (1, 0, 2)), class_sums)


def solution(mesh):
    return jax.shard_map(
        functools.partial(local, mesh.shape["ref"], mesh.shape["dom"]),
        mesh=mesh,
        in_specs=(
            P(("ref", "dom"), None),
            P(("ref", "dom")),
            P("ref", None),
            P(),
            P(),
            P(),
            P(),
            P(),
        ),
        out_specs=(P(("ref", "dom"), None, None), P(None, ("ref", "dom"))),
        check_vma=False,
    )
```

```python
import functools
import math

import jax
import jax.numpy as jnp
import numpy as np
from jax import lax
from jax.experimental import pallas as pl
from jax.experimental.pallas import tpu as pltpu
from jax.sharding import PartitionSpec as P


SHIFTS = 9
PAIRS = 4
LANES = 128
CHUNK = 512
VMEM_LIMIT = 24 * 1024 * 1024


def turning_table(count):
    coeffs = np.arange(count)
    column_freq = (coeffs % 56).astype(np.float32)
    row_freq = (coeffs // 56 - 32).astype(np.float32)
    shift_ids = np.arange(SHIFTS - PAIRS, SHIFTS)
    right = (shift_ids % 3 - 1).astype(np.float32)
    down = (shift_ids // 3 - 1).astype(np.float32)
    turning = np.float32(2.0 * math.pi / 96.0) * (
        right[:, None] * column_freq[None, :] + down[:, None] * row_freq[None, :]
    )
    return np.concatenate([np.cos(turning), np.sin(turning)], axis=0).astype(np.float32)


def odd_bits(value):
    return bin(value).count("1") % 2


def mask_of(group):
    return 2 * group + odd_bits(group)


def chunks(total):
    size = CHUNK if total % CHUNK == 0 else LANES
    return [(start, size) for start in range(0, total, size)]


def dot_nt(left, right):
    return lax.dot_general(
        left, right, (((1,), (1,)), ((), ())), preferred_element_type=jnp.float32
    )


def two_parts(value):
    high = value.astype(jnp.bfloat16)
    low = (value - high.astype(jnp.float32)).astype(jnp.bfloat16)
    return [high, low]


def cross_terms(ref_blocks, part_ref, table_ref, weight_ref, want_norm, arriving=()):
    rows, width = part_ref.shape
    coefs = width // 2
    count = sum(block.shape[0] for block in ref_blocks)
    cross = jnp.zeros((SHIFTS * rows, count), jnp.float32)
    norm = jnp.zeros((count, LANES), jnp.float32)
    middle = SHIFTS // 2
    for i, (start, size) in enumerate(chunks(coefs)):
        for copy in arriving[i] if arriving else ():
            copy.wait()
        re = pl.ds(start, size)
        im = pl.ds(coefs + start, size)
        row = start // LANES
        weight = jnp.concatenate(
            [weight_ref[row + j : row + j + 1, :] for j in range(size // LANES)], axis=1
        )
        twice = 2.0 * weight
        table = table_ref[:, re] * twice
        x = part_ref[:, re].astype(jnp.float32)
        y = part_ref[:, im].astype(jnp.float32)
        real = [None] * SHIFTS
        imag = [None] * SHIFTS
        real[middle] = (x * twice).astype(jnp.bfloat16)
        imag[middle] = (y * twice).astype(jnp.bfloat16)
        for p in range(PAIRS):
            cosine = table[p : p + 1]
            sine = table[PAIRS + p : PAIRS + p + 1]
            xc, ys, xs, yc = x * cosine, y * sine, x * sine, y * cosine
            t = middle + 1 + p
            real[t] = (xc - ys).astype(jnp.bfloat16)
            imag[t] = (xs + yc).astype(jnp.bfloat16)
            real[SHIFTS - 1 - t] = (xc + ys).astype(jnp.bfloat16)
            imag[SHIFTS - 1 - t] = (yc - xs).astype(jnp.bfloat16)
        refs_re = jnp.concatenate([block[:, re] for block in ref_blocks], axis=0)
        refs_im = jnp.concatenate([block[:, im] for block in ref_blocks], axis=0)
        cross += dot_nt(jnp.concatenate(real, axis=0), refs_re)
        cross += dot_nt(jnp.concatenate(imag, axis=0), refs_im)
        if want_norm:
            for lane in range(0, size, LANES):
                a = refs_re[:, lane : lane + LANES].astype(jnp.float32)
                b = refs_im[:, lane : lane + LANES].astype(jnp.float32)
                norm += weight[:, lane : lane + LANES] * (a * a + b * b)
    return cross, norm


def block_prior(index, class_ref, orient_ref, class_prior_ref, orient_prior_ref):
    kind = class_ref[pl.ds(index, 1), :]
    orient = orient_ref[pl.ds(index, 1), :]
    first = jnp.zeros(kind.shape, jnp.float32)
    second = jnp.zeros(kind.shape, jnp.float32)
    for c in range(class_prior_ref.shape[0]):
        first = jnp.where(kind == c, class_prior_ref[c], first)
    for o in range(orient_prior_ref.shape[0]):
        second = jnp.where(orient == o, orient_prior_ref[o], second)
    return first + second


def statistics(classes, me, blocks, class_ref, tag):
    scores = jnp.concatenate(blocks, axis=1)
    rows = scores.shape[0] // SHIFTS
    peak = scores[:rows]
    for t in range(1, SHIFTS):
        peak = jnp.maximum(peak, scores[t * rows : (t + 1) * rows])
    peak = jnp.max(peak, axis=1, keepdims=True)
    mass = jnp.exp(scores - jnp.concatenate([peak] * SHIFTS, axis=0))
    kind = jnp.concatenate(
        [class_ref[pl.ds(me, 1), :], class_ref[pl.ds(lax.bitwise_xor(me, 1), 1), :]], axis=1
    )
    want = lax.rem(lax.broadcasted_iota(jnp.int32, (LANES, scores.shape[1]), 0), classes)
    table = jnp.where(want == kind, 1.0, 0.0).astype(jnp.bfloat16)
    span = SHIFTS * rows
    by_class = dot_nt(jnp.concatenate(two_parts(mass), axis=0), table)
    by_class = by_class[:span] + by_class[span:]
    lane = lax.broadcasted_iota(jnp.int32, (rows, LANES), 1)
    shift = lane // classes
    stats = jnp.where(lane == SHIFTS * classes, peak, 0.0)
    if tag is not None:
        stats = jnp.where(lane == SHIFTS * classes + 1, tag, stats)
    for t in range(SHIFTS):
        stats = jnp.where(shift == t, by_class[t * rows : (t + 1) * rows], stats)
    return stats


def near_body(refs_hbm, part_hbm, table_hbm, weight_hbm, class_hbm, orient_hbm,
              class_prior_hbm, orient_prior_hbm, offset_hbm, scores_ref, bias_ref, tag_ref,
              refs_ref, part_ref, table_ref, weight_ref, class_ref,
              orient_ref, class_prior_ref, orient_prior_ref, offset_ref, small_sems, refs_sems):
    me = lax.axis_index("ref")
    coefs = part_ref.shape[1] // 2
    small = [
        pltpu.make_async_copy(source, target, small_sems.at[i])
        for i, (source, target) in enumerate(
            [
                (part_hbm, part_ref), (table_hbm, table_ref), (weight_hbm, weight_ref),
                (class_hbm, class_ref), (orient_hbm, orient_ref),
                (class_prior_hbm, class_prior_ref), (orient_prior_hbm, orient_prior_ref),
                (offset_hbm, offset_ref),
            ]
        )
    ]
    for copy in small:
        copy.start()
    arriving = []
    for i, (start, size) in enumerate(chunks(coefs)):
        pair = []
        for j in range(2):
            columns = pl.ds(j * coefs + start, size)
            pair.append(
                pltpu.make_async_copy(
                    refs_hbm.at[:, columns], refs_ref.at[:, columns], refs_sems.at[2 * i + j]
                )
            )
        for copy in pair:
            copy.start()
        arriving.append(pair)
    for copy in small:
        copy.wait()
    rows = part_ref.shape[0]
    row = lax.broadcasted_iota(jnp.int32, (rows, LANES), 0)
    tag = jnp.zeros((rows, LANES), jnp.int32)
    for i in range(rows):
        tag = jnp.where(row == i, offset_ref[i], tag)
    tag_ref[...] = tag.astype(jnp.float32)
    cross, norm = cross_terms([refs_ref], part_ref, table_ref, weight_ref, True, arriving)
    priors = [
        block_prior(
            lax.bitwise_xor(me, i), class_ref, orient_ref, class_prior_ref, orient_prior_ref
        )
        for i in range(2)
    ]
    bias = priors[0] - jnp.sum(jnp.transpose(norm), axis=0, keepdims=True)
    bias_ref[0:1, :] = bias
    bias_ref[1:2, :] = priors[1]
    scores_ref[...] = (cross + bias).reshape(scores_ref.shape)


def pair_body(classes, near_ref, peer_ref, part_ref, table_ref, weight_ref, class_ref, prior_ref,
              tag_ref, scores_ref, bias_ref, stats_ref):
    me = lax.axis_index("ref")
    cross, norm = cross_terms([peer_ref], part_ref, table_ref, weight_ref, True)
    bias = prior_ref[1:2, :] - jnp.sum(jnp.transpose(norm), axis=0, keepdims=True)
    bias_ref[0:1, :] = prior_ref[0:1, :]
    bias_ref[1:2, :] = bias
    scores = cross + bias
    scores_ref[...] = scores.reshape(scores_ref.shape)
    near = near_ref[...].reshape(scores.shape)
    stats_ref[...] = statistics(classes, me, [near, scores], class_ref, tag_ref[...])


def far_body(classes, own_ref, peer_ref, part_ref, table_ref, weight_ref, class_ref, bias_ref,
             scores_ref, stats_ref):
    me = lax.axis_index("ref")
    block = own_ref.shape[0]
    cross, _ = cross_terms([own_ref, peer_ref], part_ref, table_ref, weight_ref, False)
    blocks = [cross[:, i * block : (i + 1) * block] + bias_ref[i : i + 1, :] for i in range(2)]
    stats_ref[...] = statistics(classes, me, blocks, class_ref, None)
    for i in range(2):
        scores_ref[:, :, i * block : (i + 1) * block] = blocks[i].reshape(
            scores_ref.shape[0], scores_ref.shape[1], block
        )


VMEM = pl.BlockSpec(memory_space=pltpu.VMEM)
HBM = pl.BlockSpec(memory_space=pltpu.HBM)


def call(body, shapes, specs, cost, *operands, scratch=()):
    return pl.pallas_call(
        body,
        out_shape=[
            shape if isinstance(shape, jax.ShapeDtypeStruct)
            else jax.ShapeDtypeStruct(shape, jnp.float32)
            for shape in shapes
        ],
        scratch_shapes=scratch,
        in_specs=specs,
        out_specs=[VMEM] * len(shapes),
        compiler_params=pltpu.CompilerParams(vmem_limit_bytes=VMEM_LIMIT),
        cost_estimate=pl.CostEstimate(
            flops=int(cost * 5e8), bytes_accessed=int(cost * 1e6), transcendentals=0
        ),
    )(*operands)


def sums_body(groups, classes, scale, table_ref, *refs):
    stats = refs[:groups]
    parts = refs[groups : 2 * groups]
    sums_ref, total_ref = refs[2 * groups :]
    rows = parts[0].shape[0]
    width = parts[0].shape[1]
    coefs = width // 2
    span = width // groups
    used = SHIFTS * classes
    me = lax.axis_index("ref")
    dom = lax.axis_index("dom")
    chip, core = me // 2, lax.rem(me, 2)
    lane = lax.broadcasted_iota(jnp.int32, (rows, LANES), 1)
    shift = lane // classes
    right = (shift % 3 - 1).astype(jnp.float32)
    down = (shift // 3 - 1).astype(jnp.float32)
    posts = []
    for slot in range(groups):
        seen = [stats[i][(slot ^ i) * rows : ((slot ^ i) + 1) * rows] for i in range(groups)]
        peaks = [value[:, used : used + 1] for value in seen]
        peak = functools.reduce(jnp.maximum, peaks)
        mass = sum(value * jnp.exp(low - peak) for value, low in zip(seen, peaks))
        centre = stats[slot][:rows, used + 1 : used + 2].astype(jnp.int32)
        across = right - (centre % 3 - 1).astype(jnp.float32)
        along = down - (centre // 3 - 1).astype(jnp.float32)
        prior = -0.5 * (across * across + along * along)
        mass = jnp.where(lane < used, mass * jnp.exp(prior), 0.0)
        whole = jnp.sum(mass, axis=1, keepdims=True)
        posts.append(mass / whole)
        if slot == 0:
            total_ref[...] = prior - (peak + jnp.log(whole))
    post = jnp.transpose(jnp.concatenate(posts, axis=0)) * scale
    middle = SHIFTS // 2
    by_shift = [post[t * classes : (t + 1) * classes] for t in range(SHIFTS)]
    even = [by_shift[middle]]
    odd = []
    sign = jnp.where(chip < groups // 2, -1.0, 1.0)
    for p in range(PAIRS):
        t = middle + 1 + p
        even.append(by_shift[t] + by_shift[SHIFTS - 1 - t])
        odd.append(sign * (by_shift[t] - by_shift[SHIFTS - 1 - t]))
    even = jnp.concatenate(two_parts(jnp.concatenate(even, axis=0)), axis=0)
    odd = jnp.concatenate(two_parts(jnp.concatenate(odd, axis=0)), axis=0)
    column = chip * span
    other = lax.rem(column + coefs, width)
    base = lax.rem(column, coefs)
    step = CHUNK if span % CHUNK == 0 else LANES
    ne = (PAIRS + 1) * classes
    no = PAIRS * classes
    pieces = []
    for start in range(0, span, step):
        u = jnp.concatenate(
            [part[:, pl.ds(pl.multiple_of(column + start, LANES), step)] for part in parts], axis=0
        )
        v = jnp.concatenate(
            [part[:, pl.ds(pl.multiple_of(other + start, LANES), step)] for part in parts], axis=0
        )
        table = table_ref[:, pl.ds(pl.multiple_of(base + start, LANES), step)]
        evens = jnp.dot(even, u, preferred_element_type=jnp.float32)
        odds = jnp.dot(odd, v, preferred_element_type=jnp.float32)
        evens = evens[:ne] + evens[ne:]
        odds = odds[:no] + odds[no:]
        result = evens[:classes]
        for p in range(PAIRS):
            result += table[p : p + 1] * evens[(p + 1) * classes : (p + 2) * classes]
            result += table[PAIRS + p : PAIRS + p + 1] * odds[p * classes : (p + 1) * classes]
        pieces.append(result)
    result = jnp.concatenate(pieces, axis=1)
    slots = sums_ref.shape[1]
    columns = sums_ref.shape[3]
    side, rest = core, dom
    for _ in range(slots.bit_length() - 1):
        side, rest = lax.bitwise_xor(side, lax.rem(rest, 2)), rest // 2
    for half in range(2):
        for d in range(slots):
            at = (half * slots + d) * columns
            sums_ref[lax.bitwise_xor(side, half ^ odd_bits(d)), lax.bitwise_xor(dom, d)] = result[
                :, at : at + columns
            ]


def order_body(block, groups, masks, total_ref, *refs):
    out_ref = refs[-1]
    me = lax.axis_index("ref")
    slot = 0
    for ref in refs[:-1]:
        for at in range(0, ref.shape[2], block):
            place = pl.multiple_of(lax.bitwise_xor(me, masks[slot]) * block, LANES)
            for t in range(SHIFTS):
                lift = total_ref[:, t * groups : t * groups + 1]
                out_ref[t, :, pl.ds(place, block)] = ref[t, :, at : at + block] + lift
            slot += 1


def local(refs_axis, dom_axis, particles, offsets, references, noise_weight, ref_class, ref_orient,
          class_logprior, orient_logprior):
    rows, width = particles.shape
    coefs = width // 2
    block = references.shape[0]
    classes = class_logprior.shape[0]
    groups = refs_axis // 2
    me = lax.axis_index("ref")

    def swap(value, ref_mask, dom_mask):
        pairs = [
            (r * dom_axis + d, (r ^ ref_mask) * dom_axis + (d ^ dom_mask))
            for r in range(refs_axis)
            for d in range(dom_axis)
        ]
        return lax.ppermute(value, ("ref", "dom"), pairs)

    others = [swap(particles, mask_of(i), 0) for i in range(1, groups)]
    peer_refs = swap(references, 1, 0)

    table = jnp.asarray(turning_table(coefs))
    weight = noise_weight.reshape(coefs // LANES, LANES)
    kinds = ref_class.reshape(refs_axis, block)
    orients = ref_orient.reshape(refs_axis, block)
    loaded = [references, particles, table, weight, kinds]
    near, prior, tag, *held = call(
        near_body,
        [(SHIFTS, rows, block), (2, block), (rows, LANES)]
        + [jax.ShapeDtypeStruct(value.shape, value.dtype) for value in loaded],
        [HBM] * 9,
        1.0,
        *[pltpu.with_memory_space_constraint(v, pltpu.HBM) for v in [*loaded, orients, class_logprior, orient_logprior, offsets]],
        scratch=[
            pltpu.VMEM(orients.shape, jnp.int32),
            pltpu.SMEM(class_logprior.shape, jnp.float32),
            pltpu.SMEM(orient_logprior.shape, jnp.float32),
            pltpu.SMEM(offsets.shape, jnp.int32),
            pltpu.SemaphoreType.DMA((8,)),
            pltpu.SemaphoreType.DMA((2 * len(chunks(coefs)),)),
        ],
    )
    held_refs, held_part, table, weight, kinds = held
    shared = (table, weight, kinds)
    pair, bias, own_stats = call(
        functools.partial(pair_body, classes),
        [(SHIFTS, rows, block), (2, block), (rows, LANES)],
        [VMEM] * 8,
        1.0,
        near, peer_refs, held_part, *shared, prior, tag,
    )
    sent_scores, stats = [], [own_stats]
    for other in others:
        value, stat = call(
            functools.partial(far_body, classes),
            [(SHIFTS, rows, 2 * block), (rows, LANES)],
            [VMEM] * 7,
            1.0,
            held_refs, peer_refs, other, *shared, bias,
        )
        sent_scores.append(value)
        stats.append(stat)
    stats = jnp.concatenate(stats, axis=0)
    seen = [stats] + [swap(stats, mask_of(i), 0) for i in range(1, groups)]
    got = [swap(value, mask_of(i + 1), 0) for i, value in enumerate(sent_scores)]
    devices = refs_axis * dom_axis
    sums, total = call(
        functools.partial(sums_body, groups, classes, 1.0 / math.sqrt(rows * devices)),
        [(2, dom_axis, classes, width // devices), (rows, LANES)],
        [VMEM] * (1 + 2 * groups),
        1.0,
        table, *seen, held_part, *others,
    )
    keep = sums[0] + swap(sums[1], 1, 0)
    slots = dom_axis
    while slots > 1:
        slots //= 2
        keep = keep[:slots] + swap(keep[slots:], 1, slots)
    class_sums = keep[0]

    blocks = [near, pair] + got
    masks = [mask_of(i) ^ j for i in range(groups) for j in range(2)]
    if block % LANES == 0:
        (log_post,) = call(
            functools.partial(order_body, block, classes, masks),
            [(SHIFTS, rows, refs_axis * block)],
            [VMEM] * (1 + len(blocks)),
            0.5,
            total, *blocks,
        )
    else:
        pieces = [near, pair]
        for value in got:
            pieces += [value[:, :, :block], value[:, :, block:]]
        pieces = [pieces[masks.index(j)] for j in range(refs_axis)]
        bit = 1
        while bit < refs_axis:
            pieces = [
                jnp.where((me & bit) != 0, pieces[j ^ bit], pieces[j]) for j in range(refs_axis)
            ]
            bit *= 2
        lift = total[:, : SHIFTS * classes : classes].T
        log_post = jnp.concatenate(pieces, axis=2) + lift[:, :, None]
    return (jnp.transpose(log_post, (1, 0, 2)), class_sums)


def solution(mesh):
    def body(*args):
        return local(mesh.shape["ref"], mesh.shape["dom"], *args)

    return jax.shard_map(
        body,
        mesh=mesh,
        in_specs=(
            P(("ref", "dom"), None),
            P(("ref", "dom")),
            P("ref", None),
            P(),
            P(),
            P(),
            P(),
            P(),
        ),
        out_specs=(P(("ref", "dom"), None, None), P(None, ("ref", "dom"))),
        check_vma=False,
    )
```
